32 devices in a mesh: expert: 8 (over z, x), dp: 4 (over y, core).
Axes of the slice: x: 2, y: 2, z: 4, core: 2. Of those that a mesh axis runs over, the one named last changes fastest.
Arguments:
- tokens: bfloat16 [8192, 1024], P(('expert', 'dp')), may hold values from -6 to 6
- route_ids: int32 [8192, 2], P(('expert', 'dp')), may hold values from 0 to 7, all different within a row; in each aligned block of 256 rows (0 to 255, 256 to 511, ...) at most 96 rows name the same one
- gate_values: float32 [8192, 2], P(('expert', 'dp')), may hold values from 0.2 to 1
- w_gate: bfloat16 [8, 1024, 1024], P('expert', 'dp'), may hold values from -0.1875 to 0.1875
- w_up: bfloat16 [8, 1024, 1024], P('expert', 'dp'), may hold values from -0.1875 to 0.1875
- w_down: bfloat16 [8, 1024, 1024], P('expert', 'dp'), may hold values from -0.1875 to 0.1875
- swap_flags: int32 [8], replicated, may hold values from 0 to 1, as said below
- out_grad: bfloat16 [8192, 1024], P(('expert', 'dp')), may hold values from -6 to 6
Outputs:
- layer_out: bfloat16 [8192, 1024], P(('expert', 'dp'))
- grad_tokens: bfloat16 [8192, 1024], P(('expert', 'dp'))
- grad_gate: float32 [8, 1024, 1024], P('expert', 'dp')
- grad_up: float32 [8, 1024, 1024], P('expert', 'dp')
- grad_down: float32 [8, 1024, 1024], P('expert', 'dp')
The draws below stay inside these ranges and needn't reach their ends.
Inputs may be any that keep to these rules, and one draw needn't show every extreme that they name: `route_ids`: within the rows of one device (256 tokens) no expert is named by more than 96 token-expert pairs, a bound that some block reaches; a token's 2 experts differ. `swap_flags`: the first and the last pair always exchange their experts.
All inputs are finite; a program needn't handle non-finite values.
Results may differ from the reference program's by a relative error of at most 0.012.
Values may be sent and summed in bfloat16 or wider, within the bound.
A program may use at most 64 MiB of HBM per device.

```python
import math
import jax
import jax.numpy as jnp
import numpy as np
from jax import lax

D = 1024
F = 1024
EXP_DEV = 1
TOP = 2
TOK_DEV = 256
EXPERTS = 8
CAP = 96
TOKENS = 8192
SWAP_PAIRS = 4
N_EXPERT = 8
N_DP = 4


def draw_swap_flags(key, part):
    flag_bits = jax.random.randint(key, (N_EXPERT,), 0, 2).astype(jnp.int32)
    flag_bits = flag_bits.at[0].set(1 - flag_bits[SWAP_PAIRS])
    flag_bits = flag_bits.at[SWAP_PAIRS - 1].set(1 - flag_bits[N_EXPERT - 1])
    return flag_bits.astype(jnp.int32)


def level_of(own_key, extent, pieces, smallest, top_value):
    level, own = 1.0, jax.random.fold_in(own_key, 6)
    for axis_at, parts in pieces:
        heights = jnp.exp(jax.random.uniform(jax.random.fold_in(own, axis_at), (parts,), jnp.float32, smallest / len(pieces), top_value / len(pieces)))
        level = level * jnp.repeat(heights, extent[axis_at] // parts).reshape([-1 if axis == axis_at else 1 for axis in range(len(extent))])
    return level


def deal_out(rng, own, number, rows, count, top, most, skew):
    sequence = jax.random.permutation(rng, count)
    packed, ordinary = load_shares(count, rows * top, most, skew, True), load_shares(count, rows * top, most, skew, False)
    places = jnp.arange(count)

    def named(tallies, turn):
        used = int((tallies > 0).sum())
        fixed = max(1, used // 4)
        shifted = fixed + (places - fixed + turn * (used - fixed)) % max(1, count - fixed)
        return jnp.zeros((count,), jnp.int32).at[sequence[jnp.where(places < fixed, places, shifted)]].set(jnp.asarray(tallies, jnp.int32))

    tallies = jnp.where(number % 4 == 0, named(packed, number // 4), named(ordinary, number - number // 4 - 1))
    mixed = jax.random.permutation(jax.random.fold_in(own, 3), count)
    source_of, sink = mixed[0:count // 2 * 2:2], mixed[1:count // 2 * 2:2]
    slack = jnp.minimum(tallies[source_of] - 1, most - tallies[sink]) // 2
    slack = jnp.where((source_of == sequence[0]) | (sink == sequence[0]) | (tallies[sink] == 0), 0, jnp.maximum(slack, 0))
    shifted = jax.random.randint(jax.random.fold_in(own, 4), (count // 2,), 0, 1 << 20) % (slack + 1)
    tallies = tallies.at[source_of].add(-shifted).at[sink].add(shifted)
    items = jnp.searchsorted(jnp.cumsum(tallies), jnp.arange(rows * top), side="right").astype(jnp.int32)
    listing = items.reshape(top, rows).T
    listing = listing[jax.random.permutation(jax.random.fold_in(own, 1), rows)]
    turn = jax.random.randint(jax.random.fold_in(own, 2), (rows, 1), 0, top)
    return jnp.take_along_axis(listing, (jnp.arange(top)[None, :] + turn) % top, axis=1)


def load_shares(count, total, most, skew, full):
    portions = [(1 << 20) // math.isqrt(standing ** skew) + 1 for standing in range(1, count + 1)]
    largest = most if full else min(most, max(-(-total // count), total * portions[0] // sum(portions)))
    least = 1 if total - largest >= count - 1 else 0
    holding, rest = [largest] + [least] * (count - 1), total - largest - least * (count - 1)
    while rest > 0:
        movable = [i for i in range(1, count) if holding[i] < largest] or [i for i in range(1, count) if holding[i] < most]
        pool, budget = sum([portions[i] for i in movable]), rest
        for i in movable:
            addition = min(most - holding[i], max(1, budget * portions[i] // pool), rest)
            holding[i] = holding[i] + addition
            rest = rest - addition
    return np.array(holding)


def centred(own_key, shape, width, limit, cuts=(), kind=jnp.bfloat16):
    gain = level_of(own_key, shape, cuts, -0.22, 0.18) if cuts else 1.0
    array = jax.random.normal(own_key, shape, jnp.float32) * width * gain
    return jnp.minimum(jnp.maximum(array, -limit), limit).astype(kind)


def setup_inputs(seed: int = 0) -> dict:
    keys = jax.random.split(jax.random.key(seed), 9)
    tokens = centred(keys[0], (TOKENS, D), 1.0, 6.0, ((0, 32),))
    route_ids_keys = jax.random.split(jax.random.fold_in(keys[1], 1), TOKENS // TOK_DEV)
    route_ids_turns = jax.random.permutation(jax.random.fold_in(keys[1], 3), TOKENS // TOK_DEV)
    route_ids = jax.vmap(lambda own, number: deal_out(jax.random.fold_in(keys[1], 2), own, number, TOK_DEV, EXPERTS, TOP, CAP, 1))(route_ids_keys, route_ids_turns).reshape((TOKENS, TOP))
    gate_values = jnp.clip(0.2 + 0.8 * jax.random.uniform(keys[2], (TOKENS, TOP), jnp.float32) ** level_of(keys[2], (TOKENS, TOP), ((0, 32),), -0.2, 0.2), 0.2, 1.0)
    w_gate = centred(keys[3], (EXPERTS, D, F), D ** -0.5, 0.1875, ((0, 8), (1, 4)))
    w_up = centred(keys[4], (EXPERTS, D, F), D ** -0.5, 0.1875, ((0, 8), (1, 4)))
    w_down = centred(keys[5], (EXPERTS, F, D), F ** -0.5, 0.1875, ((0, 8), (1, 4)))
    swap_flags = draw_swap_flags(jax.random.fold_in(keys[8], 71), 0)
    out_grad = centred(keys[7], (TOKENS, D), 1.0, 6.0, ((0, 32),))
    return {"tokens": tokens, "route_ids": route_ids, "gate_values": gate_values, "w_gate": w_gate, "w_up": w_up, "w_down": w_down, "swap_flags": swap_flags, "out_grad": out_grad}


def round_half(values):
    return lax.optimization_barrier(values.astype(jnp.bfloat16)).astype(jnp.float32)


def reference(tokens, route_ids, gate_values, w_gate, w_up, w_down, swap_flags, out_grad):
    blocks = N_EXPERT * N_DP
    experts = EXP_DEV * N_EXPERT
    copies = TOK_DEV * TOP
    route_rows = route_ids.reshape(blocks, copies)
    onehot = (route_rows[:, :, None] == jnp.arange(experts, dtype=jnp.int32)[None, None, :]).astype(jnp.int32)
    rank_of = jnp.sum(jnp.cumsum(onehot, axis=1) * onehot, axis=2) - 1
    block_ids = jnp.broadcast_to(jnp.arange(blocks, dtype=jnp.int32)[:, None], (blocks, copies))
    copy_ids = jnp.broadcast_to(jnp.arange(copies, dtype=jnp.int32)[None, :], (blocks, copies))
    slot_table = jnp.full((blocks, experts, CAP), -1, jnp.int32).at[block_ids, route_rows, rank_of].set(copy_ids)
    gate_rows = gate_values.reshape(blocks, copies).astype(jnp.float32)
    column_ids = jnp.arange(blocks, dtype=jnp.int32)[:, None]

    def one_expert(totals, expert):
        mixed_sum, token_sum = totals
        rows_of = slot_table[:, expert, :]
        is_live = rows_of >= 0
        copy_pick = jnp.maximum(rows_of, 0)
        token_pick = (column_ids * TOK_DEV + copy_pick // TOP).reshape(-1)
        gate_pick = jnp.where(is_live, gate_rows[column_ids, copy_pick], 0.0).reshape(-1, 1)
        live_col = is_live.reshape(-1, 1)
        token_in = jnp.where(live_col, tokens[token_pick].astype(jnp.float32), 0.0)
        cot_in = round_half(gate_pick * out_grad[token_pick].astype(jnp.float32))
        gate_w = w_gate[expert].astype(jnp.float32)
        up_w = w_up[expert].astype(jnp.float32)
        down_w = w_down[expert].astype(jnp.float32)
        pre_gate = jnp.dot(token_in, gate_w)
        pre_up = jnp.dot(token_in, up_w)
        hidden = round_half(jax.nn.silu(pre_gate) * pre_up)
        expert_out = round_half(jnp.dot(hidden, down_w))
        mixed_sum = mixed_sum.at[token_pick].add(gate_pick * expert_out)
        grad_h = jnp.dot(cot_in, down_w.T)
        sigmoid_a = jax.nn.sigmoid(pre_gate)
        grad_a = round_half(grad_h * pre_up * sigmoid_a * (1.0 + pre_gate * (1.0 - sigmoid_a)))
        grad_b = round_half(grad_h * pre_gate * sigmoid_a)
        copy_grad = round_half(jnp.dot(grad_a, gate_w.T) + jnp.dot(grad_b, up_w.T))
        token_sum = token_sum.at[token_pick].add(copy_grad)
        token_four = token_in.reshape(N_EXPERT, N_DP, CAP, D)
        hidden_four = hidden.reshape(N_EXPERT, N_DP, CAP, F)
        cot_four = cot_in.reshape(N_EXPERT, N_DP, CAP, D)
        part_gate = round_half(jnp.einsum('idcx,idcf->dxf', token_four, grad_a.reshape(N_EXPERT, N_DP, CAP, F)))
        part_up = round_half(jnp.einsum('idcx,idcf->dxf', token_four, grad_b.reshape(N_EXPERT, N_DP, CAP, F)))
        part_down = round_half(jnp.einsum('idcf,idcx->dfx', hidden_four, cot_four))
        return (mixed_sum, token_sum), (jnp.sum(part_gate, axis=0), jnp.sum(part_up, axis=0), jnp.sum(part_down, axis=0))

    start_sums = (jnp.zeros((TOKENS, D), jnp.float32), jnp.zeros((TOKENS, D), jnp.float32))
    (mixed_sum, token_sum), stacked = lax.scan(one_expert, start_sums, jnp.arange(experts, dtype=jnp.int32))
    expert_ids = jnp.arange(experts, dtype=jnp.int32)
    owner = expert_ids // EXP_DEV
    pair_of = owner % SWAP_PAIRS
    paired = swap_flags[pair_of] != swap_flags[pair_of + SWAP_PAIRS]
    holder = jnp.where(paired, (owner + SWAP_PAIRS) % N_EXPERT, owner)
    slot_of = (holder * EXP_DEV + expert_ids % EXP_DEV).astype(jnp.int32)
    return (mixed_sum.astype(jnp.bfloat16), token_sum.astype(jnp.bfloat16), stacked[0][slot_of], stacked[1][slot_of], stacked[2][slot_of])
```

```python
import functools

import jax
import jax.numpy as jnp
from jax import lax
from jax.experimental import pallas as pl
from jax.experimental.pallas import tpu as pltpu
from jax.sharding import Mesh, PartitionSpec as P

BF = jnp.bfloat16
F32 = jnp.float32
MESH = pl.DeviceIdType.MESH
TILE = 256


def dot(a, b, a_dim, b_dim):
    return lax.dot_general(a, b, (((a_dim,), (b_dim,)), ((), ())), preferred_element_type=F32)


def tile_at(j, size):
    return pl.ds(pl.multiple_of(j * size, size), size)


def kernel(
    nl, nr, cap, flags, tokens, route, gates, out_grad, in_gate, in_up, in_down,
    layer_out, grad_tokens, out_gate, out_up, out_down,
    pick, send_x, send_c, recv_x, recv_c, x_t, h_t, w_gate, w_up, w_down, relay,
    pre_gate, pre_up, hidden, grad_a, grad_b, dw_down, dw_gate, dw_up, from_r, from_y, to_z, from_z,
    send_out, send_grad, ret_out, ret_grad,
    z_s, z_r, y_s, y_r, w_s, w_r, g_s, g_r, d_s, d_r, own_sem,
):
    h, l, b, r = (lax.axis_index(name) for name in ("h", "l", "b", "r"))
    experts = 2 * nl
    rows, n_f = in_gate.shape
    tok = tokens.shape[0]
    slots = experts * cap
    me = b * nl + l
    early = h == b
    late = h != b
    z_dev, y_dev = (1 - h, l, b, r), (h, l, 1 - b, r)
    ins, full = (in_gate, in_up, in_down), (w_gate, w_up, w_down)

    def remote(src, dst, send_sem, recv_sem, dev):
        return pltpu.make_async_remote_copy(
            src_ref=src, dst_ref=dst, send_sem=send_sem, recv_sem=recv_sem,
            device_id=dev, device_id_type=MESH,
        )

    def q_dev(q):
        return (h, lax.rem(q, nl), q // nl, r)

    def r_peer(p):
        return lax.rem(r + p, nr)

    def r_from(p):
        return lax.rem(r + nr - p, nr)

    def shard(side, rest):
        return tile_at(side * nr + rest, rows)

    barrier = pltpu.get_barrier_semaphore()
    peers = [z_dev] + [(h, l, b, r_peer(p)) for p in range(1, nr)]
    peers += [q_dev(lax.rem(me + p, experts)) for p in range(1, experts)]
    for dev in peers:
        pl.semaphore_signal(barrier, inc=1, device_id=dev, device_id_type=MESH)
    pl.semaphore_wait(barrier, len(peers))

    def z_weight(w, dst):
        return remote(ins[w], dst, z_s.at[w], z_r.at[w], z_dev)

    def y_weight(w, src, side):
        return remote(src, full[w].at[shard(side, r)], y_s.at[w], y_r.at[w], y_dev)

    def r_weight(w, group, src, side, p, rest):
        return remote(
            src, full[w].at[shard(side, rest)], w_s.at[w, group, p - 1], w_r.at[w, group, p - 1],
            (h, l, b, r_peer(p)),
        )

    def own_copy(w):
        return pltpu.make_async_copy(ins[w], full[w].at[shard(b, r)], own_sem.at[w])

    def weight_start(w):
        @pl.when(early)
        def _():
            z_weight(w, full[w].at[shard(b, r)]).start()
            own_copy(w).start()
            for p in range(1, nr):
                r_weight(w, 0, ins[w], b, p, r).start()

        @pl.when(late)
        def _():
            z_weight(w, relay.at[w]).start()
            y_weight(w, ins[w], b).start()

    def weight_z(w):
        @pl.when(early)
        def _():
            z_weight(w, relay.at[w]).wait_recv()
            y_weight(w, relay.at[w], b).start()

        @pl.when(late)
        def _():
            z_weight(w, full[w].at[shard(b, r)]).wait_recv()
            for p in range(1, nr):
                r_weight(w, 0, full[w].at[shard(b, r)], b, p, r).start()

    def weight_y(w):
        mine = full[w].at[shard(1 - b, r)]
        y_weight(w, mine, 1 - b).wait_recv()
        for p in range(1, nr):
            r_weight(w, 1, mine, 1 - b, p, r).start()

    def weight_r(w):
        for p in range(1, nr):
            r_weight(w, 0, ins[w], b, p, r_from(p)).wait_recv()
            r_weight(w, 1, ins[w], 1 - b, p, r_from(p)).wait_recv()

        @pl.when(early)
        def _():
            own_copy(w).wait()

    def rows_of(q):
        return tile_at(q, cap)

    def exchange(k, src, dst, p, sender):
        q = lax.rem(me + p, experts)
        return remote(
            src.at[rows_of(q)], dst.at[rows_of(sender)], d_s.at[k, p - 1], d_r.at[k, p - 1], q_dev(q)
        )

    def exchange_start(k, src, dst):
        for p in range(1, experts):
            exchange(k, src, dst, p, me).start()
        dst[rows_of(me), :] = src[rows_of(me), :]

    def exchange_wait(k, src, dst):
        for p in range(1, experts):
            exchange(k, src, dst, p, lax.rem(me + experts - p, experts)).wait_recv()

    parts = (dw_gate, dw_up, dw_down)
    first_flag, second_flag = flags[l], flags[l + nl]
    final_side = jnp.where(first_flag != second_flag, 1 - h, h)
    keep_mine = jnp.where(final_side == b, 1.0, 0.0).astype(F32)

    def r_grad(w, p, side):
        return remote(
            parts[w].at[shard(side, r_peer(p))], from_r.at[w, p - 1, side],
            g_s.at[w, p - 1, side], g_r.at[w, p - 1, side], (h, l, b, r_peer(p)),
        )

    def y_grad(w):
        return remote(parts[w].at[shard(1 - b, r)], from_y.at[w], y_s.at[3 + w], y_r.at[3 + w], y_dev)

    def z_grad(w):
        return remote(to_z.at[w], from_z.at[w], z_s.at[3 + w], z_r.at[3 + w], z_dev)

    def grad_r_start(w):
        for side in range(2):
            for p in range(1, nr):
                r_grad(w, p, side).start()

    chunk = min(rows, 64)

    def grad_sum(w):
        for side in range(2):
            for p in range(1, nr):
                r_grad(w, p, side).wait_recv()

        for side in range(2):
            @pl.loop(0, rows // chunk)
            def _(i):
                at = pl.ds(pl.multiple_of((side * nr + r) * rows + i * chunk, chunk), chunk)
                near = tile_at(i, chunk)
                total = parts[w][at, :].astype(F32)
                for p in range(1, nr):
                    total = total + from_r[w, p - 1, side, near, :].astype(F32)
                parts[w][at, :] = total.astype(BF)
        y_grad(w).start()

    def sides(w, i):
        at = pl.ds(pl.multiple_of((b * nr + r) * rows + i * chunk, chunk), chunk)
        return parts[w][at, :].astype(F32), from_y[w, tile_at(i, chunk), :].astype(F32)

    def grad_z_start(w):
        y_grad(w).wait_recv()

        @pl.loop(0, rows // chunk)
        def _(i):
            mine, other = sides(w, i)
            to_z[w, tile_at(i, chunk), :] = (mine * (1.0 - keep_mine) + other * keep_mine).astype(BF)
        z_grad(w).start()

    def grad_end(w, out):
        z_grad(w).wait_recv()

        @pl.loop(0, rows // chunk)
        def _(i):
            mine, other = sides(w, i)
            kept = mine * keep_mine + other * (1.0 - keep_mine)
            out[tile_at(i, chunk), :] = kept + from_z[w, tile_at(i, chunk), :].astype(F32)

    weight_start(0)

    lanes = lax.broadcasted_iota(jnp.int32, (tok, 128), 1)
    one, two = route[:, 0:1], route[:, 1:2]
    match_one, match_two = one == lanes, two == lanes
    named = (jnp.where(match_one, 1.0, 0.0) + jnp.where(match_two, 1.0, 0.0)).astype(BF)
    row_id = lax.broadcasted_iota(jnp.int32, (tok, tok), 0)
    col_id = lax.broadcasted_iota(jnp.int32, (tok, tok), 1)
    before = dot(jnp.where(col_id < row_id, 1.0, 0.0).astype(BF), named, 1, 0)
    slot_ids = lax.broadcasted_iota(jnp.int32, (tok, slots), 1)
    for k, (ids, match) in enumerate(((one, match_one), (two, match_two))):
        rank = jnp.sum(jnp.where(match, before, 0.0), axis=1, keepdims=True).astype(jnp.int32)
        pick[k] = jnp.where(ids * cap + rank == slot_ids, 1.0, 0.0).astype(BF)
    both = pick[0] + pick[1]

    n_tiles = n_f // TILE
    d_tiles = tokens.shape[1] // TILE
    chosen = both.astype(F32).T.astype(BF)

    @pl.loop(0, d_tiles)
    def _(j):
        send_x[:, tile_at(j, TILE)] = dot(chosen, tokens[:, tile_at(j, TILE)], 1, 0).astype(BF)

    exchange_start(0, send_x, recv_x)
    weight_start(1)
    one_t, two_t = pick[0].astype(F32).T.astype(BF), pick[1].astype(F32).T.astype(BF)

    @pl.loop(0, d_tiles)
    def _(j):
        cot = out_grad[:, tile_at(j, TILE)].astype(F32)
        cot_one = (gates[:, 0:1] * cot).astype(BF)
        cot_two = (gates[:, 1:2] * cot).astype(BF)
        send_c[:, tile_at(j, TILE)] = (dot(one_t, cot_one, 1, 0) + dot(two_t, cot_two, 1, 0)).astype(BF)

    weight_z(0)
    exchange_start(1, send_c, recv_c)
    weight_start(2)
    weight_y(0)
    weight_r(0)
    exchange_wait(0, send_x, recv_x)

    @pl.loop(0, n_tiles)
    def _(j):
        at = tile_at(j, TILE)
        pre_gate[:, at] = dot(recv_x[...], w_gate[:, at], 1, 0)

    @pl.loop(0, d_tiles)
    def _(j):
        at = tile_at(j, TILE)
        x_t[at, :] = recv_x[:, at].T

    weight_z(1)
    weight_y(1)
    weight_r(1)

    @pl.loop(0, n_tiles)
    def _(j):
        at = tile_at(j, TILE)
        up = dot(recv_x[...], w_up[:, at], 1, 0)
        gate = pre_gate[:, at]
        pre_up[:, at] = up
        hid = (gate * jax.nn.sigmoid(gate) * up).astype(BF)
        hidden[:, at] = hid
        h_t[at, :] = hid.T

    exchange_wait(1, send_c, recv_c)

    @pl.loop(0, d_tiles)
    def _(j):
        at = tile_at(j, TILE)
        dw_down[:, at] = dot(h_t[...], recv_c[:, at], 1, 0).astype(BF)

    grad_r_start(2)
    weight_z(2)
    grad_sum(2)
    weight_y(2)
    weight_r(2)

    @pl.loop(0, n_tiles)
    def _(j):
        at = tile_at(j, TILE)
        grad_h = dot(recv_c[...], w_down[at, :], 1, 1)
        gate, up = pre_gate[:, at], pre_up[:, at]
        sig = jax.nn.sigmoid(gate)
        grad_a[:, at] = (grad_h * up * sig * (1.0 + gate * (1.0 - sig))).astype(BF)
        grad_b[:, at] = (grad_h * gate * sig).astype(BF)

    grad_z_start(2)

    @pl.loop(0, n_tiles)
    def _(j):
        at = tile_at(j, TILE)
        dw_gate[:, at] = dot(x_t[...], grad_a[:, at], 1, 0).astype(BF)

    grad_r_start(0)

    @pl.loop(0, n_tiles)
    def _(j):
        at = tile_at(j, TILE)
        dw_up[:, at] = dot(x_t[...], grad_b[:, at], 1, 0).astype(BF)

    grad_r_start(1)
    grad_sum(0)
    grad_sum(1)

    @pl.loop(0, d_tiles)
    def _(j):
        at = tile_at(j, TILE)
        send_out[:, at] = dot(hidden[...], w_down[:, at], 1, 0).astype(BF)

    exchange_start(2, send_out, ret_out)

    @pl.loop(0, d_tiles)
    def _(j):
        at = tile_at(j, TILE)
        send_grad[:, at] = (dot(grad_a[...], w_gate[at, :], 1, 1) + dot(grad_b[...], w_up[at, :], 1, 1)).astype(BF)

    grad_z_start(0)
    exchange_start(3, send_grad, ret_grad)
    grad_z_start(1)
    exchange_wait(2, send_out, ret_out)

    @pl.loop(0, d_tiles)
    def _(j):
        at = tile_at(j, TILE)
        layer_out[:, at] = (
            gates[:, 0:1] * dot(pick[0], ret_out[:, at], 1, 0)
            + gates[:, 1:2] * dot(pick[1], ret_out[:, at], 1, 0)
        ).astype(BF)

    grad_end(2, out_down)
    exchange_wait(3, send_grad, ret_grad)

    @pl.loop(0, d_tiles)
    def _(j):
        at = tile_at(j, TILE)
        grad_tokens[:, at] = dot(pick[0] + pick[1], ret_grad[:, at], 1, 0).astype(BF)

    grad_end(0, out_gate)
    grad_end(1, out_up)

    for w in range(3):
        z_weight(w, relay.at[w]).wait_send()
        y_weight(w, ins[w], b).wait_send()
        z_grad(w).wait_send()
        y_grad(w).wait_send()
        for p in range(1, nr):
            for group in range(2):
                r_weight(w, group, ins[w], b, p, r).wait_send()
                r_grad(w, p, group).wait_send()
    for k, (src, dst) in enumerate(
        ((send_x, recv_x), (send_c, recv_c), (send_out, ret_out), (send_grad, ret_grad))
    ):
        for p in range(1, experts):
            exchange(k, src, dst, p, me).wait_send()


def shards(tokens, route_ids, gate_values, w_gate, w_up, w_down, swap_flags, out_grad):
    nl, nr = lax.axis_size("l"), lax.axis_size("r")
    tok, width = tokens.shape
    rows, n_f = w_gate.shape[1:]
    cap = 3 * tok * route_ids.shape[1] // (4 * nl)
    slots = 2 * nl * cap
    wide = 2 * nr * rows
    vmem = pl.BlockSpec(memory_space=pltpu.VMEM)
    hbm = pl.BlockSpec(memory_space=pl.ANY)
    dma = pltpu.SemaphoreType.DMA
    slot_rows = pltpu.VMEM((slots, width), BF)
    slot_f32 = pltpu.VMEM((slots, n_f), F32)
    weight = pltpu.VMEM((wide, n_f), BF)
    step = pl.pallas_call(
        functools.partial(kernel, nl, nr, cap),
        out_shape=(
            jax.ShapeDtypeStruct((tok, width), BF),
            jax.ShapeDtypeStruct((tok, width), BF),
            jax.ShapeDtypeStruct((rows, n_f), F32),
            jax.ShapeDtypeStruct((rows, n_f), F32),
            jax.ShapeDtypeStruct((rows, n_f), F32),
        ),
        in_specs=[pl.BlockSpec(memory_space=pltpu.SMEM), vmem, vmem, vmem, vmem, hbm, hbm, hbm],
        out_specs=(vmem,) * 5,
        scratch_shapes=[
            pltpu.VMEM((2, tok, slots), BF),
            slot_rows, slot_rows, slot_rows, slot_rows,
            pltpu.VMEM((width, slots), BF), pltpu.VMEM((n_f, slots), BF),
            weight, weight, weight,
            pltpu.VMEM((3, rows, n_f), BF),
            slot_f32, slot_f32,
            slot_rows, slot_rows, slot_rows,
            weight, weight, weight,
            pltpu.VMEM((3, nr - 1, 2, rows, n_f), BF),
            pltpu.VMEM((3, rows, n_f), BF),
            pltpu.VMEM((3, rows, n_f), BF),
            pltpu.VMEM((3, rows, n_f), BF),
            slot_rows, slot_rows, slot_rows, slot_rows,
            dma((6,)), dma((6,)), dma((6,)), dma((6,)),
            dma((3, 2, nr - 1)), dma((3, 2, nr - 1)),
            dma((3, nr - 1, 2)), dma((3, nr - 1, 2)),
            dma((4, 2 * nl - 1)), dma((4, 2 * nl - 1)),
            dma((3,)),
        ],
        compiler_params=pltpu.CompilerParams(
            collective_id=0, has_side_effects=True, vmem_limit_bytes=67043328
        ),
    )
    outs = step(swap_flags, tokens, route_ids, gate_values, out_grad, w_gate[0], w_up[0], w_down[0])
    return outs[0], outs[1], outs[2][None], outs[3][None], outs[4][None]


def solution(mesh):
    n_expert, n_dp = mesh.shape["expert"], mesh.shape["dp"]
    split = Mesh(mesh.devices.reshape(2, n_expert // 2, 2, n_dp // 2), ("h", "l", "b", "r"))
    rows = P(("h", "l", "b", "r"), None)
    weight = P(("h", "l"), ("b", "r"), None)
    return jax.shard_map(
        shards,
        mesh=split,
        in_specs=(rows, rows, rows, weight, weight, weight, P(), rows),
        out_specs=(rows, rows, weight, weight, weight),
        check_vma=False,
    )
```

```python
import functools

import jax
import jax.numpy as jnp
from jax import lax
from jax.experimental import pallas as pl
from jax.experimental.pallas import tpu as pltpu
from jax.sharding import Mesh, PartitionSpec as P

BF = jnp.bfloat16
F32 = jnp.float32
MESH = pl.DeviceIdType.MESH
TILE = 256


def dot(a, b, a_dim, b_dim):
    return lax.dot_general(a, b, (((a_dim,), (b_dim,)), ((), ())), preferred_element_type=F32)


def tile_at(j, size):
    return pl.ds(pl.multiple_of(j * size, size), size)


def kernel(
    nl, nr, cap, flags, tokens, route_t, gates_t, out_grad, in_gate, in_up, in_down,
    layer_out, grad_tokens, out_gate, out_up, out_down,
    pick, send_x, send_c, recv_x, recv_c, x_t, h_t, w_gate, w_up, w_down, relay,
    pre_gate, pre_up, hidden, grad_a, grad_b, dw_down, dw_gate, dw_up, from_r, from_y, to_z, from_z,
    send_out, send_grad, ret_out, ret_grad, gates,
    z_s, z_r, y_s, y_r, w_s, w_r, g_s, g_r, d_s, d_r, own_sem,
):
    h, l, b, r = (lax.axis_index(name) for name in ("h", "l", "b", "r"))
    experts = 2 * nl
    rows, n_f = in_gate.shape
    tok = tokens.shape[0]
    slots = experts * cap
    me = b * nl + l
    early = h == b
    late = h != b
    z_dev, y_dev = (1 - h, l, b, r), (h, l, 1 - b, r)
    ins, full = (in_gate, in_up, in_down), (w_gate, w_up, w_down)

    def remote(src, dst, send_sem, recv_sem, dev):
        return pltpu.make_async_remote_copy(
            src_ref=src, dst_ref=dst, send_sem=send_sem, recv_sem=recv_sem,
            device_id=dev, device_id_type=MESH,
        )

    def q_dev(q):
        return (h, lax.rem(q, nl), q // nl, r)

    def r_peer(p):
        return lax.rem(r + p, nr)

    def r_from(p):
        return lax.rem(r + nr - p, nr)

    def shard(side, rest):
        return tile_at(side * nr + rest, rows)

    barrier = pltpu.get_barrier_semaphore()
    peers = [z_dev] + [(h, l, b, r_peer(p)) for p in range(1, nr)]
    peers += [q_dev(lax.rem(me + p, experts)) for p in range(1, experts)]
    for dev in peers:
        pl.semaphore_signal(barrier, inc=1, device_id=dev, device_id_type=MESH)
    pl.semaphore_wait(barrier, len(peers))

    def z_weight(w, dst):
        return remote(ins[w], dst, z_s.at[w], z_r.at[w], z_dev)

    def y_weight(w, src, side):
        return remote(src, full[w].at[shard(side, r)], y_s.at[w], y_r.at[w], y_dev)

    def r_weight(w, group, src, side, p, rest):
        return remote(
            src, full[w].at[shard(side, rest)], w_s.at[w, group, p - 1], w_r.at[w, group, p - 1],
            (h, l, b, r_peer(p)),
        )

    def own_copy(w):
        return pltpu.make_async_copy(ins[w], full[w].at[shard(b, r)], own_sem.at[w])

    def weight_start(w):
        @pl.when(early)
        def _():
            z_weight(w, full[w].at[shard(b, r)]).start()
            own_copy(w).start()
            for p in range(1, nr):
                r_weight(w, 0, ins[w], b, p, r).start()

        @pl.when(late)
        def _():
            z_weight(w, relay.at[w]).start()
            y_weight(w, ins[w], b).start()

    def weight_z(w):
        @pl.when(early)
        def _():
            z_weight(w, relay.at[w]).wait_recv()
            y_weight(w, relay.at[w], b).start()

        @pl.when(late)
        def _():
            z_weight(w, full[w].at[shard(b, r)]).wait_recv()
            for p in range(1, nr):
                r_weight(w, 0, full[w].at[shard(b, r)], b, p, r).start()

    def weight_y(w):
        mine = full[w].at[shard(1 - b, r)]
        y_weight(w, mine, 1 - b).wait_recv()
        for p in range(1, nr):
            r_weight(w, 1, mine, 1 - b, p, r).start()

    def weight_r(w):
        for p in range(1, nr):
            r_weight(w, 0, ins[w], b, p, r_from(p)).wait_recv()
            r_weight(w, 1, ins[w], 1 - b, p, r_from(p)).wait_recv()

        @pl.when(early)
        def _():
            own_copy(w).wait()

    def rows_of(q):
        return tile_at(q, cap)

    def exchange(k, src, dst, p, sender):
        q = lax.rem(b + p // nl, 2) * nl + lax.rem(l + p % nl, nl)
        return remote(
            src.at[rows_of(q)], dst.at[rows_of(sender)], d_s.at[k, p - 1], d_r.at[k, p - 1], q_dev(q)
        )

    def exchange_start(k, src, dst, across):
        for p in range(nl, experts) if across else range(1, nl):
            exchange(k, src, dst, p, me).start()
        if not across:
            dst[rows_of(me), :] = src[rows_of(me), :]

    def exchange_wait(k, src, dst):
        for p in range(1, experts):
            sender = lax.rem(b + p // nl, 2) * nl + lax.rem(l + nl - p % nl, nl)
            exchange(k, src, dst, p, sender).wait_recv()

    parts = (dw_gate, dw_up, dw_down)
    first_flag, second_flag = flags[l], flags[l + nl]
    final_side = jnp.where(first_flag != second_flag, 1 - h, h)
    keep_mine = jnp.where(final_side == b, 1.0, 0.0).astype(F32)

    def r_grad(w, p, side):
        return remote(
            parts[w].at[shard(side, r_peer(p))], from_r.at[w, p - 1, side],
            g_s.at[w, p - 1, side], g_r.at[w, p - 1, side], (h, l, b, r_peer(p)),
        )

    def y_grad(w):
        return remote(parts[w].at[shard(1 - b, r)], from_y.at[w], y_s.at[3 + w], y_r.at[3 + w], y_dev)

    def z_grad(w):
        return remote(to_z.at[w], from_z.at[w], z_s.at[3 + w], z_r.at[3 + w], z_dev)

    def grad_r_start(w):
        for side in range(2):
            for p in range(1, nr):
                r_grad(w, p, side).start()

    chunk = min(rows, 64)

    def grad_sum(w):
        for side in range(2):
            for p in range(1, nr):
                r_grad(w, p, side).wait_recv()

        for side in range(2):
            @pl.loop(0, rows // chunk)
            def _(i):
                at = pl.ds(pl.multiple_of((side * nr + r) * rows + i * chunk, chunk), chunk)
                near = tile_at(i, chunk)
                total = parts[w][at, :].astype(F32)
                for p in range(1, nr):
                    total = total + from_r[w, p - 1, side, near, :].astype(F32)
                parts[w][at, :] = total.astype(BF)

    def sides(w, i):
        at = pl.ds(pl.multiple_of((b * nr + r) * rows + i * chunk, chunk), chunk)
        return parts[w][at, :].astype(F32), from_y[w, tile_at(i, chunk), :].astype(F32)

    def grad_z_start(w):
        y_grad(w).wait_recv()

        @pl.loop(0, rows // chunk)
        def _(i):
            mine, other = sides(w, i)
            to_z[w, tile_at(i, chunk), :] = (mine * (1.0 - keep_mine) + other * keep_mine).astype(BF)
        z_grad(w).start()

    def grad_end(w, out):
        z_grad(w).wait_recv()

        @pl.loop(0, rows // chunk)
        def _(i):
            mine, other = sides(w, i)
            kept = mine * keep_mine + other * (1.0 - keep_mine)
            out[tile_at(i, chunk), :] = kept + from_z[w, tile_at(i, chunk), :].astype(F32)

    weight_start(0)

    row_id = lax.broadcasted_iota(jnp.int32, (tok, tok), 0)
    col_id = lax.broadcasted_iota(jnp.int32, (tok, tok), 1)

    def column(line):
        return jnp.sum(jnp.where(row_id == col_id, line, 0.0), axis=1, keepdims=True)

    for k in range(2):
        gates[:, k : k + 1] = column(gates_t[k : k + 1, :])
    one, two = (column(route_t[k : k + 1, :].astype(F32)).astype(jnp.int32) for k in range(2))
    lanes = lax.broadcasted_iota(jnp.int32, (tok, 128), 1)
    match_one, match_two = one == lanes, two == lanes
    named = (jnp.where(match_one, 1.0, 0.0) + jnp.where(match_two, 1.0, 0.0)).astype(BF)
    before = dot(jnp.where(col_id < row_id, 1.0, 0.0).astype(BF), named, 1, 0)
    slot_ids = lax.broadcasted_iota(jnp.int32, (tok, slots), 1)
    for k, (ids, match) in enumerate(((one, match_one), (two, match_two))):
        rank = jnp.sum(jnp.where(match, before, 0.0), axis=1, keepdims=True).astype(jnp.int32)
        pick[k] = jnp.where(ids * cap + rank == slot_ids, 1.0, 0.0).astype(BF)
    both = pick[0] + pick[1]

    n_tiles = n_f // TILE
    d_tiles = tokens.shape[1] // TILE
    chosen = both.astype(F32).T.astype(BF)

    @pl.loop(0, d_tiles)
    def _(j):
        send_x[:, tile_at(j, TILE)] = dot(chosen, tokens[:, tile_at(j, TILE)], 1, 0).astype(BF)

    exchange_start(0, send_x, recv_x, False)
    exchange_start(0, send_x, recv_x, True)
    weight_start(1)
    one_t, two_t = pick[0].astype(F32).T.astype(BF), pick[1].astype(F32).T.astype(BF)

    @pl.loop(0, d_tiles)
    def _(j):
        cot = out_grad[:, tile_at(j, TILE)].astype(F32)
        cot_one = (gates[:, 0:1] * cot).astype(BF)
        cot_two = (gates[:, 1:2] * cot).astype(BF)
        send_c[:, tile_at(j, TILE)] = (dot(one_t, cot_one, 1, 0) + dot(two_t, cot_two, 1, 0)).astype(BF)

    weight_z(0)
    exchange_start(1, send_c, recv_c, False)
    exchange_start(1, send_c, recv_c, True)
    weight_start(2)
    weight_y(0)
    weight_r(0)
    exchange_wait(0, send_x, recv_x)

    @pl.loop(0, n_tiles)
    def _(j):
        at = tile_at(j, TILE)
        pre_gate[:, at] = dot(recv_x[...], w_gate[:, at], 1, 0)

    @pl.loop(0, d_tiles)
    def _(j):
        at = tile_at(j, TILE)
        x_t[at, :] = recv_x[:, at].T

    weight_z(1)
    weight_y(1)
    weight_r(1)

    @pl.loop(0, n_tiles)
    def _(j):
        at = tile_at(j, TILE)
        up = dot(recv_x[...], w_up[:, at], 1, 0)
        gate = pre_gate[:, at]
        pre_up[:, at] = up
        hid = (gate * jax.nn.sigmoid(gate) * up).astype(BF)
        hidden[:, at] = hid
        h_t[at, :] = hid.T

    exchange_wait(1, send_c, recv_c)

    @pl.loop(0, d_tiles)
    def _(j):
        at = tile_at(j, TILE)
        dw_down[:, at] = dot(h_t[...], recv_c[:, at], 1, 0).astype(BF)

    grad_r_start(2)
    weight_z(2)
    grad_sum(2)
    y_grad(2).start()
    weight_y(2)
    weight_r(2)

    @pl.loop(0, n_tiles)
    def _(j):
        at = tile_at(j, TILE)
        grad_h = dot(recv_c[...], w_down[at, :], 1, 1)
        gate, up = pre_gate[:, at], pre_up[:, at]
        sig = jax.nn.sigmoid(gate)
        grad_a[:, at] = (grad_h * up * sig * (1.0 + gate * (1.0 - sig))).astype(BF)
        grad_b[:, at] = (grad_h * gate * sig).astype(BF)

    @pl.loop(0, d_tiles)
    def _(j):
        at = tile_at(j, TILE)
        send_out[:, at] = dot(hidden[...], w_down[:, at], 1, 0).astype(BF)

    exchange_start(2, send_out, ret_out, False)

    @pl.loop(0, n_tiles)
    def _(j):
        at = tile_at(j, TILE)
        dw_gate[:, at] = dot(x_t[...], grad_a[:, at], 1, 0).astype(BF)

    grad_r_start(0)
    grad_z_start(2)
    grad_sum(0)
    y_grad(0).start()

    @pl.loop(0, n_tiles)
    def _(j):
        at = tile_at(j, TILE)
        dw_up[:, at] = dot(x_t[...], grad_b[:, at], 1, 0).astype(BF)

    grad_r_start(1)

    @pl.loop(0, d_tiles)
    def _(j):
        at = tile_at(j, TILE)
        send_grad[:, at] = (dot(grad_a[...], w_gate[at, :], 1, 1) + dot(grad_b[...], w_up[at, :], 1, 1)).astype(BF)

    exchange_start(3, send_grad, ret_grad, False)
    grad_sum(1)
    y_grad(0).wait_send()
    y_grad(1).start()
    grad_z_start(0)

    y_grad(1).wait_send()
    exchange_start(2, send_out, ret_out, True)
    exchange_start(3, send_grad, ret_grad, True)
    grad_z_start(1)
    exchange_wait(2, send_out, ret_out)

    @pl.loop(0, d_tiles)
    def _(j):
        at = tile_at(j, TILE)
        layer_out[:, at] = (
            gates[:, 0:1] * dot(pick[0], ret_out[:, at], 1, 0)
            + gates[:, 1:2] * dot(pick[1], ret_out[:, at], 1, 0)
        ).astype(BF)

    grad_end(2, out_down)
    exchange_wait(3, send_grad, ret_grad)

    @pl.loop(0, d_tiles)
    def _(j):
        at = tile_at(j, TILE)
        grad_tokens[:, at] = dot(pick[0] + pick[1], ret_grad[:, at], 1, 0).astype(BF)

    grad_end(0, out_gate)
    grad_end(1, out_up)

    y_grad(2).wait_send()
    for w in range(3):
        z_weight(w, relay.at[w]).wait_send()
        y_weight(w, ins[w], b).wait_send()
        z_grad(w).wait_send()
        for p in range(1, nr):
            for group in range(2):
                r_weight(w, group, ins[w], b, p, r).wait_send()
                r_grad(w, p, group).wait_send()
    for k, (src, dst) in enumerate(
        ((send_x, recv_x), (send_c, recv_c), (send_out, ret_out), (send_grad, ret_grad))
    ):
        for p in range(1, experts):
            exchange(k, src, dst, p, me).wait_send()


def store(*refs):
    sems = refs[-1]
    copies = [pltpu.make_async_copy(refs[i], refs[5 + i], sems.at[i]) for i in range(5)]
    for copy in copies:
        copy.start()
    for copy in copies:
        copy.wait()


def shards(tokens, route_ids, gate_values, w_gate, w_up, w_down, swap_flags, out_grad):
    nl, nr = lax.axis_size("l"), lax.axis_size("r")
    tok, width = tokens.shape
    rows, n_f = w_gate.shape[1:]
    cap = 3 * tok * route_ids.shape[1] // (4 * nl)
    slots = 2 * nl * cap
    wide = 2 * nr * rows
    vmem = pl.BlockSpec(memory_space=pltpu.VMEM)
    hbm = pl.BlockSpec(memory_space=pl.ANY)
    dma = pltpu.SemaphoreType.DMA
    slot_rows = pltpu.VMEM((slots, width), BF)
    slot_f32 = pltpu.VMEM((slots, n_f), F32)
    weight = pltpu.VMEM((wide, n_f), BF)
    step = pl.pallas_call(
        functools.partial(kernel, nl, nr, cap),
        out_shape=(
            jax.ShapeDtypeStruct((tok, width), BF),
            jax.ShapeDtypeStruct((tok, width), BF),
            jax.ShapeDtypeStruct((rows, n_f), F32),
            jax.ShapeDtypeStruct((rows, n_f), F32),
            jax.ShapeDtypeStruct((rows, n_f), F32),
        ),
        in_specs=[pl.BlockSpec(memory_space=pltpu.SMEM), vmem, vmem, vmem, vmem, hbm, hbm, hbm],
        out_specs=(vmem,) * 5,
        scratch_shapes=[
            pltpu.VMEM((2, tok, slots), BF),
            slot_rows, slot_rows, slot_rows, slot_rows,
            pltpu.VMEM((width, slots), BF), pltpu.VMEM((n_f, slots), BF),
            weight, weight, weight,
            pltpu.VMEM((3, rows, n_f), BF),
            slot_f32, slot_f32,
            slot_rows, slot_rows, slot_rows,
            weight, weight, weight,
            pltpu.VMEM((3, nr - 1, 2, rows, n_f), BF),
            pltpu.VMEM((3, rows, n_f), BF),
            pltpu.VMEM((3, rows, n_f), BF),
            pltpu.VMEM((3, rows, n_f), BF),
            slot_rows, slot_rows, slot_rows, slot_rows,
            pltpu.VMEM((tok, 2), F32),
            dma((6,)), dma((6,)), dma((6,)), dma((6,)),
            dma((3, 2, nr - 1)), dma((3, 2, nr - 1)),
            dma((3, nr - 1, 2)), dma((3, nr - 1, 2)),
            dma((4, 2 * nl - 1)), dma((4, 2 * nl - 1)),
            dma((3,)),
        ],
        compiler_params=pltpu.CompilerParams(
            collective_id=0, has_side_effects=True, vmem_limit_bytes=67043328
        ),
    )
    outs = step(swap_flags, tokens, route_ids.T, gate_values.T, out_grad, w_gate[0], w_up[0], w_down[0])
    outs = pl.pallas_call(
        store,
        out_shape=tuple(jax.ShapeDtypeStruct(out.shape, out.dtype) for out in outs),
        in_specs=[vmem] * 5,
        out_specs=(hbm,) * 5,
        scratch_shapes=[dma((5,))],
    )(*outs)
    return outs[0], outs[1], outs[2][None], outs[3][None], outs[4][None]


def solution(mesh):
    n_expert, n_dp = mesh.shape["expert"], mesh.shape["dp"]
    split = Mesh(mesh.devices.reshape(2, n_expert // 2, 2, n_dp // 2), ("h", "l", "b", "r"))
    rows = P(("h", "l", "b", "r"), None)
    weight = P(("h", "l"), ("b", "r"), None)
    return jax.shard_map(
        shards,
        mesh=split,
        in_specs=(rows, rows, rows, weight, weight, weight, P(), rows),
        out_specs=(rows, rows, weight, weight, weight),
        check_vma=False,
    )
```

```python
import functools

import jax
import jax.numpy as jnp
from jax import lax
from jax.experimental import pallas as pl
from jax.experimental.pallas import tpu as pltpu
from jax.sharding import Mesh, PartitionSpec as P

BF = jnp.bfloat16
F32 = jnp.float32
MESH = pl.DeviceIdType.MESH
TILE = 256
PIECES = 2


def dot(a, b, a_dim, b_dim):
    return lax.dot_general(a, b, (((a_dim,), (b_dim,)), ((), ())), preferred_element_type=F32)


def tile_at(j, size):
    return pl.ds(pl.multiple_of(j * size, size), size)


def kernel(
    nl, nr, cap, flags, tokens, route_t, gates_t, out_grad, in_gate, in_up, in_down,
    layer_out, grad_tokens, out_gate, out_up, out_down,
    pick, send_x, send_c, recv_x, recv_c, x_t, h_t, w_gate, w_up, w_down, relay,
    pre_gate, pre_up, hidden, grad_a, grad_b, dw_down, dw_gate, dw_up, from_r, from_y, to_z, from_z,
    send_out, send_grad, ret_out, ret_grad, gates, gates_far, near, far, route_p, gates_p, far_send, far_recv,
    z_s, z_r, y_s, y_r, w_s, w_r, g_s, g_r, d_s, d_r, own_sem, p_s, p_r, f_s, f_r,
):
    h, l, b, r = (lax.axis_index(name) for name in ("h", "l", "b", "r"))
    experts = 2 * nl
    rows, n_f = in_gate.shape
    tok = tokens.shape[0]
    slots = experts * cap
    me = b * nl + l
    early = h == b
    late = h != b
    z_dev, y_dev = (1 - h, l, b, r), (h, l, 1 - b, r)
    ins, full = (in_gate, in_up, in_down), (w_gate, w_up, w_down)

    def remote(src, dst, send_sem, recv_sem, dev):
        return pltpu.make_async_remote_copy(
            src_ref=src, dst_ref=dst, send_sem=send_sem, recv_sem=recv_sem,
            device_id=dev, device_id_type=MESH,
        )

    def q_dev(q):
        return (h, lax.rem(q, nl), q // nl, r)

    def r_peer(p):
        return lax.rem(r + p, nr)

    def r_from(p):
        return lax.rem(r + nr - p, nr)

    def shard(side, rest):
        return tile_at(side * nr + rest, rows)

    barrier = pltpu.get_barrier_semaphore()
    peers = [z_dev] + [(h, l, b, r_peer(p)) for p in range(1, nr)]
    peers += [q_dev(lax.rem(me + p, experts)) for p in range(1, experts)]
    for dev in peers:
        pl.semaphore_signal(barrier, inc=1, device_id=dev, device_id_type=MESH)
    pl.semaphore_wait(barrier, len(peers))

    piece_rows = rows // PIECES

    def piece(i):
        return pl.ds(i * piece_rows, piece_rows)

    def shard_piece(side, rest, i):
        return pl.ds(pl.multiple_of((side * nr + rest) * rows + i * piece_rows, piece_rows), piece_rows)

    def z_weight(w, i, dst):
        return remote(ins[w].at[piece(i)], dst, z_s.at[w, i], z_r.at[w, i], z_dev)

    def y_weight(w, i, src, side):
        return remote(src, full[w].at[shard_piece(side, r, i)], y_s.at[w, i], y_r.at[w, i], y_dev)

    def r_weight(w, i, group, src, side, p, rest):
        return remote(
            src, full[w].at[shard_piece(side, rest, i)],
            w_s.at[w, i, group, p - 1], w_r.at[w, i, group, p - 1], (h, l, b, r_peer(p)),
        )

    def own_copy(w):
        return pltpu.make_async_copy(ins[w], full[w].at[shard(b, r)], own_sem.at[w])

    def weight_start(w):
        @pl.when(early)
        def _():
            for i in range(PIECES):
                z_weight(w, i, full[w].at[shard_piece(b, r, i)]).start()
            own_copy(w).start()
            for i in range(PIECES):
                for p in range(1, nr):
                    r_weight(w, i, 0, ins[w].at[piece(i)], b, p, r).start()

        @pl.when(late)
        def _():
            for i in range(PIECES):
                z_weight(w, i, relay.at[w, piece(i)]).start()
                y_weight(w, i, ins[w].at[piece(i)], b).start()

    def weight_z(w, i):
        @pl.when(early)
        def _():
            z_weight(w, i, relay.at[w, piece(i)]).wait_recv()
            y_weight(w, i, relay.at[w, piece(i)], b).start()

        @pl.when(late)
        def _():
            mine = full[w].at[shard_piece(b, r, i)]
            z_weight(w, i, mine).wait_recv()
            for p in range(1, nr):
                r_weight(w, i, 0, mine, b, p, r).start()

    def weight_y(w):
        for i in range(PIECES):
            mine = full[w].at[shard_piece(1 - b, r, i)]
            y_weight(w, i, mine, 1 - b).wait_recv()
            for p in range(1, nr):
                r_weight(w, i, 1, mine, 1 - b, p, r).start()

    def weight_r(w):
        for i in range(PIECES):
            for p in range(1, nr):
                r_weight(w, i, 0, ins[w].at[piece(i)], b, p, r_from(p)).wait_recv()
                r_weight(w, i, 1, ins[w].at[piece(i)], 1 - b, p, r_from(p)).wait_recv()

        @pl.when(early)
        def _():
            own_copy(w).wait()

    def rows_of(q):
        return tile_at(q, cap)

    def exchange(k, src, dst, p, sender):
        q = lax.rem(b + p // nl, 2) * nl + lax.rem(l + p % nl, nl)
        return remote(
            src.at[rows_of(q)], dst.at[rows_of(sender)], d_s.at[k, p - 1], d_r.at[k, p - 1], q_dev(q)
        )

    def exchange_start(k, src, dst, across):
        for p in range(nl, experts) if across else range(1, nl):
            exchange(k, src, dst, p, me).start()
        if not across:
            dst[rows_of(me), :] = src[rows_of(me), :]

    def exchange_wait(k, src, dst):
        for p in range(1, experts):
            sender = lax.rem(b + p // nl, 2) * nl + lax.rem(l + nl - p % nl, nl)
            exchange(k, src, dst, p, sender).wait_recv()

    def back(k, src, dst, t, dl, sender):
        at = lax.rem(l + dl, nl)
        return remote(
            src.at[rows_of(lax.rem(b + t, 2) * nl + at)], dst.at[rows_of(t * nl + sender)],
            d_s.at[k, t * nl + dl - 1], d_r.at[k, t * nl + dl - 1], (h, at, b, r),
        )

    def back_start(k, src, dst, t):
        for dl in range(1, nl):
            back(k, src, dst, t, dl, l).start()
        dst[rows_of(t * nl + l), :] = src[rows_of(lax.rem(b + t, 2) * nl + l), :]

    def back_wait(k, src, dst, t):
        for dl in range(1, nl):
            back(k, src, dst, t, dl, lax.rem(l + nl - dl, nl)).wait_recv()

    def info(i):
        return remote((route_t, gates_t)[i], (route_p, gates_p)[i], p_s.at[i], p_r.at[i], y_dev)

    def far_copy(i):
        return remote(far_send.at[i], far_recv.at[i], f_s.at[i], f_r.at[i], y_dev)

    parts = (dw_gate, dw_up, dw_down)
    first_flag, second_flag = flags[l], flags[l + nl]
    final_side = jnp.where(first_flag != second_flag, 1 - h, h)
    keep_mine = jnp.where(final_side == b, 1.0, 0.0).astype(F32)

    def r_grad(w, p, side):
        return remote(
            parts[w].at[shard(side, r_peer(p))], from_r.at[w, p - 1, side],
            g_s.at[w, p - 1, side], g_r.at[w, p - 1, side], (h, l, b, r_peer(p)),
        )

    def y_grad(w, i):
        return remote(
            parts[w].at[shard_piece(1 - b, r, i)], from_y.at[w, piece(i)],
            y_s.at[3 + w, i], y_r.at[3 + w, i], y_dev,
        )

    def y_grad_start(w):
        for i in range(PIECES):
            y_grad(w, i).start()

    def y_grad_sent(w):
        for i in range(PIECES):
            y_grad(w, i).wait_send()

    def z_grad(w, i):
        return remote(
            to_z.at[w, piece(i)], from_z.at[w, piece(i)], z_s.at[3 + w, i], z_r.at[3 + w, i], z_dev
        )

    def grad_r_start(w):
        for side in range(2):
            for p in range(1, nr):
                r_grad(w, p, side).start()

    chunk = min(piece_rows, 64)

    def grad_sum(w):
        for side in range(2):
            for p in range(1, nr):
                r_grad(w, p, side).wait_recv()

        for side in range(2):
            @pl.loop(0, rows // chunk)
            def _(i):
                at = pl.ds(pl.multiple_of((side * nr + r) * rows + i * chunk, chunk), chunk)
                near = tile_at(i, chunk)
                total = parts[w][at, :].astype(F32)
                for p in range(1, nr):
                    total = total + from_r[w, p - 1, side, near, :].astype(F32)
                parts[w][at, :] = total.astype(BF)

    def sides(w, i):
        at = pl.ds(pl.multiple_of((b * nr + r) * rows + i * chunk, chunk), chunk)
        return parts[w][at, :].astype(F32), from_y[w, tile_at(i, chunk), :].astype(F32)

    def grad_z_start(w):
        for k in range(PIECES):
            y_grad(w, k).wait_recv()

            @pl.loop(k * piece_rows // chunk, (k + 1) * piece_rows // chunk)
            def _(i):
                mine, other = sides(w, i)
                to_z[w, tile_at(i, chunk), :] = (mine * (1.0 - keep_mine) + other * keep_mine).astype(BF)
            z_grad(w, k).start()

    def grad_end(w, out):
        for k in range(PIECES):
            z_grad(w, k).wait_recv()

        @pl.loop(0, rows // chunk)
        def _(i):
            mine, other = sides(w, i)
            kept = mine * keep_mine + other * (1.0 - keep_mine)
            out[tile_at(i, chunk), :] = kept + from_z[w, tile_at(i, chunk), :].astype(F32)

    weight_start(0)

    info(0).start()
    info(1).start()
    row_id = lax.broadcasted_iota(jnp.int32, (tok, tok), 0)
    col_id = lax.broadcasted_iota(jnp.int32, (tok, tok), 1)

    def column(line):
        return jnp.sum(jnp.where(row_id == col_id, line, 0.0), axis=1, keepdims=True)

    def slots_of(lines):
        one, two = (column(lines[k : k + 1, :].astype(F32)).astype(jnp.int32) for k in range(2))
        lanes = lax.broadcasted_iota(jnp.int32, (tok, 128), 1)
        match_one, match_two = one == lanes, two == lanes
        named = (jnp.where(match_one, 1.0, 0.0) + jnp.where(match_two, 1.0, 0.0)).astype(BF)
        before = dot(jnp.where(col_id < row_id, 1.0, 0.0).astype(BF), named, 1, 0)
        places = []
        for ids, match in ((one, match_one), (two, match_two)):
            rank = jnp.sum(jnp.where(match, before, 0.0), axis=1, keepdims=True).astype(jnp.int32)
            places.append(ids * cap + rank)
        return places

    for k in range(2):
        gates[:, k : k + 1] = column(gates_t[k : k + 1, :])
    slot_ids = lax.broadcasted_iota(jnp.int32, (tok, slots), 1)
    half = nl * cap
    side_ids = lax.broadcasted_iota(jnp.int32, (tok, half), 1) + b * half
    for k, place in enumerate(slots_of(route_t)):
        pick[k] = jnp.where(place == slot_ids, 1.0, 0.0).astype(BF)
        near[k] = jnp.where(place == side_ids, 1.0, 0.0).astype(BF)
    both = pick[0] + pick[1]

    n_tiles = n_f // TILE
    d_tiles = tokens.shape[1] // TILE
    chosen = both.astype(F32).T.astype(BF)

    @pl.loop(0, d_tiles)
    def _(j):
        send_x[:, tile_at(j, TILE)] = dot(chosen, tokens[:, tile_at(j, TILE)], 1, 0).astype(BF)

    exchange_start(0, send_x, recv_x, False)
    exchange_start(0, send_x, recv_x, True)
    weight_start(1)
    one_t, two_t = pick[0].astype(F32).T.astype(BF), pick[1].astype(F32).T.astype(BF)

    @pl.loop(0, d_tiles)
    def _(j):
        cot = out_grad[:, tile_at(j, TILE)].astype(F32)
        cot_one = (gates[:, 0:1] * cot).astype(BF)
        cot_two = (gates[:, 1:2] * cot).astype(BF)
        send_c[:, tile_at(j, TILE)] = (dot(one_t, cot_one, 1, 0) + dot(two_t, cot_two, 1, 0)).astype(BF)

    exchange_start(1, send_c, recv_c, False)
    weight_z(0, 0)
    weight_z(0, 1)
    exchange_start(1, send_c, recv_c, True)
    weight_start(2)
    weight_y(0)
    weight_r(0)
    exchange_wait(0, send_x, recv_x)

    @pl.loop(0, n_tiles)
    def _(j):
        at = tile_at(j, TILE)
        pre_gate[:, at] = dot(recv_x[...], w_gate[:, at], 1, 0)

    @pl.loop(0, d_tiles)
    def _(j):
        at = tile_at(j, TILE)
        x_t[at, :] = recv_x[:, at].T

    info(0).wait_recv()
    info(1).wait_recv()
    for k in range(2):
        gates_far[:, k : k + 1] = column(gates_p[k : k + 1, :])
    for k, place in enumerate(slots_of(route_p)):
        far[k] = jnp.where(place == side_ids, 1.0, 0.0).astype(BF)

    weight_z(1, 0)
    weight_z(1, 1)
    weight_y(1)
    weight_r(1)

    @pl.loop(0, n_tiles)
    def _(j):
        at = tile_at(j, TILE)
        up = dot(recv_x[...], w_up[:, at], 1, 0)
        gate = pre_gate[:, at]
        pre_up[:, at] = up
        hid = (gate * jax.nn.sigmoid(gate) * up).astype(BF)
        hidden[:, at] = hid
        h_t[at, :] = hid.T

    weight_z(2, 0)
    exchange_wait(1, send_c, recv_c)
    weight_z(2, 1)

    @pl.loop(0, d_tiles)
    def _(j):
        at = tile_at(j, TILE)
        dw_down[:, at] = dot(h_t[...], recv_c[:, at], 1, 0).astype(BF)

    grad_r_start(2)
    grad_sum(2)
    y_grad_start(2)
    weight_y(2)
    weight_r(2)

    @pl.loop(0, n_tiles)
    def _(j):
        at = tile_at(j, TILE)
        grad_h = dot(recv_c[...], w_down[at, :], 1, 1)
        gate, up = pre_gate[:, at], pre_up[:, at]
        sig = jax.nn.sigmoid(gate)
        grad_a[:, at] = (grad_h * up * sig * (1.0 + gate * (1.0 - sig))).astype(BF)
        grad_b[:, at] = (grad_h * gate * sig).astype(BF)

    @pl.loop(0, d_tiles)
    def _(j):
        at = tile_at(j, TILE)
        send_out[:, at] = dot(hidden[...], w_down[:, at], 1, 0).astype(BF)

    back_start(2, send_out, ret_out, 1)

    @pl.loop(0, n_tiles)
    def _(j):
        at = tile_at(j, TILE)
        dw_gate[:, at] = dot(x_t[...], grad_a[:, at], 1, 0).astype(BF)

    grad_r_start(0)
    grad_z_start(2)
    grad_sum(0)
    y_grad_start(0)

    @pl.loop(0, n_tiles)
    def _(j):
        at = tile_at(j, TILE)
        dw_up[:, at] = dot(x_t[...], grad_b[:, at], 1, 0).astype(BF)

    grad_r_start(1)

    @pl.loop(0, d_tiles)
    def _(j):
        at = tile_at(j, TILE)
        send_grad[:, at] = (dot(grad_a[...], w_gate[at, :], 1, 1) + dot(grad_b[...], w_up[at, :], 1, 1)).astype(BF)

    back_start(3, send_grad, ret_grad, 1)
    back_start(2, send_out, ret_out, 0)
    back_start(3, send_grad, ret_grad, 0)
    grad_sum(1)
    y_grad_start(1)
    grad_z_start(0)
    back_wait(2, send_out, ret_out, 1)

    @pl.loop(0, d_tiles)
    def _(j):
        at = tile_at(j, TILE)
        rows_far = ret_out[half:, at]
        far_send[0, :, at] = (
            gates_far[:, 0:1] * dot(far[0], rows_far, 1, 0)
            + gates_far[:, 1:2] * dot(far[1], rows_far, 1, 0)
        ).astype(BF)

    far_copy(0).start()
    grad_z_start(1)
    back_wait(3, send_grad, ret_grad, 1)

    @pl.loop(0, d_tiles)
    def _(j):
        at = tile_at(j, TILE)
        far_send[1, :, at] = dot(far[0] + far[1], ret_grad[half:, at], 1, 0).astype(BF)

    far_copy(1).start()
    back_wait(2, send_out, ret_out, 0)

    @pl.loop(0, d_tiles)
    def _(j):
        at = tile_at(j, TILE)
        rows_near = ret_out[:half, at]
        pre_gate[:tok, at] = (
            gates[:, 0:1] * dot(near[0], rows_near, 1, 0)
            + gates[:, 1:2] * dot(near[1], rows_near, 1, 0)
        )

    back_wait(3, send_grad, ret_grad, 0)

    @pl.loop(0, d_tiles)
    def _(j):
        at = tile_at(j, TILE)
        pre_up[:tok, at] = dot(near[0] + near[1], ret_grad[:half, at], 1, 0)

    grad_end(2, out_down)
    far_copy(0).wait_recv()

    @pl.loop(0, tok // 64)
    def _(i):
        at = tile_at(i, 64)
        layer_out[at, :] = (pre_gate[at, :] + far_recv[0, at, :].astype(F32)).astype(BF)

    grad_end(0, out_gate)
    far_copy(1).wait_recv()

    @pl.loop(0, tok // 64)
    def _(i):
        at = tile_at(i, 64)
        grad_tokens[at, :] = (pre_up[at, :] + far_recv[1, at, :].astype(F32)).astype(BF)

    grad_end(1, out_up)

    for w in range(3):
        y_grad_sent(w)
    for w in range(3):
        for i in range(PIECES):
            z_weight(w, i, relay.at[w, piece(i)]).wait_send()
            y_weight(w, i, ins[w].at[piece(i)], b).wait_send()
            z_grad(w, i).wait_send()
            for p in range(1, nr):
                for group in range(2):
                    r_weight(w, i, group, ins[w].at[piece(i)], b, p, r).wait_send()
        for p in range(1, nr):
            for side in range(2):
                r_grad(w, p, side).wait_send()
    for i in range(2):
        info(i).wait_send()
        far_copy(i).wait_send()
    for k, (src, dst) in enumerate(((send_x, recv_x), (send_c, recv_c))):
        for p in range(1, experts):
            exchange(k, src, dst, p, me).wait_send()
    for k, (src, dst) in ((2, (send_out, ret_out)), (3, (send_grad, ret_grad))):
        for t in range(2):
            for dl in range(1, nl):
                back(k, src, dst, t, dl, l).wait_send()


def store(*refs):
    sems = refs[-1]
    copies = [pltpu.make_async_copy(refs[i], refs[5 + i], sems.at[i]) for i in range(5)]
    for copy in copies:
        copy.start()
    for copy in copies:
        copy.wait()


def shards(tokens, route_ids, gate_values, w_gate, w_up, w_down, swap_flags, out_grad):
    nl, nr = lax.axis_size("l"), lax.axis_size("r")
    tok, width = tokens.shape
    rows, n_f = w_gate.shape[1:]
    cap = 3 * tok * route_ids.shape[1] // (4 * nl)
    slots = 2 * nl * cap
    wide = 2 * nr * rows
    vmem = pl.BlockSpec(memory_space=pltpu.VMEM)
    hbm = pl.BlockSpec(memory_space=pl.ANY)
    dma = pltpu.SemaphoreType.DMA
    slot_rows = pltpu.VMEM((slots, width), BF)
    slot_f32 = pltpu.VMEM((slots, n_f), F32)
    weight = pltpu.VMEM((wide, n_f), BF)
    step = pl.pallas_call(
        functools.partial(kernel, nl, nr, cap),
        out_shape=(
            jax.ShapeDtypeStruct((tok, width), BF),
            jax.ShapeDtypeStruct((tok, width), BF),
            jax.ShapeDtypeStruct((rows, n_f), F32),
            jax.ShapeDtypeStruct((rows, n_f), F32),
            jax.ShapeDtypeStruct((rows, n_f), F32),
        ),
        in_specs=[pl.BlockSpec(memory_space=pltpu.SMEM), vmem, vmem, vmem, vmem, hbm, hbm, hbm],
        out_specs=(vmem,) * 5,
        scratch_shapes=[
            pltpu.VMEM((2, tok, slots), BF),
            slot_rows, slot_rows, slot_rows, slot_rows,
            pltpu.VMEM((width, slots), BF), pltpu.VMEM((n_f, slots), BF),
            weight, weight, weight,
            pltpu.VMEM((3, rows, n_f), BF),
            slot_f32, slot_f32,
            slot_rows, slot_rows, slot_rows,
            weight, weight, weight,
            pltpu.VMEM((3, nr - 1, 2, rows, n_f), BF),
            pltpu.VMEM((3, rows, n_f), BF),
            pltpu.VMEM((3, rows, n_f), BF),
            pltpu.VMEM((3, rows, n_f), BF),
            slot_rows, slot_rows, slot_rows, slot_rows,
            pltpu.VMEM((tok, 2), F32), pltpu.VMEM((tok, 2), F32),
            pltpu.VMEM((2, tok, slots // 2), BF), pltpu.VMEM((2, tok, slots // 2), BF),
            pltpu.VMEM((2, tok), jnp.int32), pltpu.VMEM((2, tok), F32),
            pltpu.VMEM((2, tok, width), BF), pltpu.VMEM((2, tok, width), BF),
            dma((6, PIECES)), dma((6, PIECES)), dma((6, PIECES)), dma((6, PIECES)),
            dma((3, PIECES, 2, nr - 1)), dma((3, PIECES, 2, nr - 1)),
            dma((3, nr - 1, 2)), dma((3, nr - 1, 2)),
            dma((4, 2 * nl - 1)), dma((4, 2 * nl - 1)),
            dma((3,)), dma((2,)), dma((2,)), dma((2,)), dma((2,)),
        ],
        compiler_params=pltpu.CompilerParams(
            collective_id=0, has_side_effects=True, vmem_limit_bytes=67043328
        ),
    )
    outs = step(swap_flags, tokens, route_ids.T, gate_values.T, out_grad, w_gate[0], w_up[0], w_down[0])
    outs = pl.pallas_call(
        store,
        out_shape=tuple(jax.ShapeDtypeStruct(out.shape, out.dtype) for out in outs),
        in_specs=[vmem] * 5,
        out_specs=(hbm,) * 5,
        scratch_shapes=[dma((5,))],
    )(*outs)
    return outs[0], outs[1], outs[2][None], outs[3][None], outs[4][None]


def solution(mesh):
    n_expert, n_dp = mesh.shape["expert"], mesh.shape["dp"]
    split = Mesh(mesh.devices.reshape(2, n_expert // 2, 2, n_dp // 2), ("h", "l", "b", "r"))
    rows = P(("h", "l", "b", "r"), None)
    weight = P(("h", "l"), ("b", "r"), None)
    return jax.shard_map(
        shards,
        mesh=split,
        in_specs=(rows, rows, rows, weight, weight, weight, P(), rows),
        out_specs=(rows, rows, weight, weight, weight),
        check_vma=False,
    )
```

```python
import functools

import jax
import jax.numpy as jnp
from jax import lax
from jax.experimental import pallas as pl
from jax.experimental.pallas import tpu as pltpu
from jax.sharding import Mesh, PartitionSpec as P

BF = jnp.bfloat16
F32 = jnp.float32
MESH = pl.DeviceIdType.MESH
TILE = 256
PIECES = 2
SPLIT = 4


def dot(a, b, a_dim, b_dim):
    return lax.dot_general(a, b, (((a_dim,), (b_dim,)), ((), ())), preferred_element_type=F32)


def tile_at(j, size):
    return pl.ds(pl.multiple_of(j * size, size), size)


def kernel(
    nl, nr, cap, flags, tokens_hbm, route_t, gates_t, out_grad_hbm, in_gate, in_up, in_down,
    layer_out, grad_tokens, out_gate, out_up, out_down,
    tokens, out_grad, io_sem, pick, send_x, send_c, recv_x, recv_c, x_t, h_t, w_gate, w_up, w_down, relay,
    pre_gate, pre_up, hidden, grad_a, grad_b, dw_down, dw_gate, dw_up, from_r, from_y, to_z, from_z,
    send_out, send_grad, ret_out, ret_grad, gates, gates_far, near, far, route_p, gates_p, far_send, far_recv,
    z_s, z_r, y_s, y_r, w_s, w_r, g_s, g_r, d_s, d_r, own_sem, p_s, p_r, f_s, f_r,
):
    def io(src, dst, i):
        return pltpu.make_async_copy(src, dst, io_sem.at[i])

    read_tokens, read_cot = io(tokens_hbm, tokens, 0), io(out_grad_hbm, out_grad, 1)
    read_tokens.start()
    read_cot.start()
    h, l, b, r = (lax.axis_index(name) for name in ("h", "l", "b", "r"))
    experts = 2 * nl
    rows, n_f = in_gate.shape
    tok = tokens.shape[0]
    slots = experts * cap
    me = b * nl + l
    early = h == b
    late = h != b
    z_dev, y_dev = (1 - h, l, b, r), (h, l, 1 - b, r)
    ins, full = (in_gate, in_up, in_down), (w_gate, w_up, w_down)

    def remote(src, dst, send_sem, recv_sem, dev):
        return pltpu.make_async_remote_copy(
            src_ref=src, dst_ref=dst, send_sem=send_sem, recv_sem=recv_sem,
            device_id=dev, device_id_type=MESH,
        )

    def q_dev(q):
        return (h, lax.rem(q, nl), q // nl, r)

    def r_peer(p):
        return lax.rem(r + p, nr)

    def r_from(p):
        return lax.rem(r + nr - p, nr)

    def shard(side, rest):
        return tile_at(side * nr + rest, rows)

    barrier = pltpu.get_barrier_semaphore()
    peers = [z_dev] + [(h, l, b, r_peer(p)) for p in range(1, nr)]
    peers += [q_dev(lax.rem(me + p, experts)) for p in range(1, experts)]
    for dev in peers:
        pl.semaphore_signal(barrier, inc=1, device_id=dev, device_id_type=MESH)
    pl.semaphore_wait(barrier, len(peers))

    piece_rows = rows // PIECES

    def piece(i):
        return pl.ds(i * piece_rows, piece_rows)

    def shard_piece(side, rest, i):
        return pl.ds(pl.multiple_of((side * nr + rest) * rows + i * piece_rows, piece_rows), piece_rows)

    def z_weight(w, i, dst):
        return remote(ins[w].at[piece(i)], dst, z_s.at[w, i], z_r.at[w, i], z_dev)

    def y_weight(w, i, src, side):
        return remote(src, full[w].at[shard_piece(side, r, i)], y_s.at[w, i], y_r.at[w, i], y_dev)

    def r_weight(w, i, group, src, side, p, rest):
        return remote(
            src, full[w].at[shard_piece(side, rest, i)],
            w_s.at[w, i, group, p - 1], w_r.at[w, i, group, p - 1], (h, l, b, r_peer(p)),
        )

    def own_copy(w):
        return pltpu.make_async_copy(ins[w], full[w].at[shard(b, r)], own_sem.at[w])

    def weight_start(w):
        @pl.when(early)
        def _():
            for i in range(PIECES):
                z_weight(w, i, full[w].at[shard_piece(b, r, i)]).start()
            own_copy(w).start()
            for i in range(PIECES):
                for p in range(1, nr):
                    r_weight(w, i, 0, ins[w].at[piece(i)], b, p, r).start()

        @pl.when(late)
        def _():
            for i in range(PIECES):
                z_weight(w, i, relay.at[w, piece(i)]).start()
                y_weight(w, i, ins[w].at[piece(i)], b).start()

    def weight_z(w, i):
        @pl.when(early)
        def _():
            z_weight(w, i, relay.at[w, piece(i)]).wait_recv()
            y_weight(w, i, relay.at[w, piece(i)], b).start()

        @pl.when(late)
        def _():
            mine = full[w].at[shard_piece(b, r, i)]
            z_weight(w, i, mine).wait_recv()
            for p in range(1, nr):
                r_weight(w, i, 0, mine, b, p, r).start()

    def weight_y(w):
        for i in range(PIECES):
            mine = full[w].at[shard_piece(1 - b, r, i)]
            y_weight(w, i, mine, 1 - b).wait_recv()
            for p in range(1, nr):
                r_weight(w, i, 1, mine, 1 - b, p, r).start()

    def weight_r(w):
        for i in range(PIECES):
            for p in range(1, nr):
                r_weight(w, i, 0, ins[w].at[piece(i)], b, p, r_from(p)).wait_recv()
                r_weight(w, i, 1, ins[w].at[piece(i)], 1 - b, p, r_from(p)).wait_recv()

        @pl.when(early)
        def _():
            own_copy(w).wait()

    def rows_of(q):
        return tile_at(q, cap)

    def exchange(k, src, dst, p, sender):
        q = lax.rem(b + p // nl, 2) * nl + lax.rem(l + p % nl, nl)
        return remote(
            src.at[rows_of(q)], dst.at[rows_of(sender)], d_s.at[k, p - 1], d_r.at[k, p - 1], q_dev(q)
        )

    def exchange_start(k, src, dst, across):
        for p in range(nl, experts) if across else range(1, nl):
            exchange(k, src, dst, p, me).start()
        if not across:
            dst[rows_of(me), :] = src[rows_of(me), :]

    def exchange_wait(k, src, dst):
        for p in range(1, experts):
            sender = lax.rem(b + p // nl, 2) * nl + lax.rem(l + nl - p % nl, nl)
            exchange(k, src, dst, p, sender).wait_recv()

    def back(k, src, dst, t, dl, sender):
        at = lax.rem(l + dl, nl)
        return remote(
            src.at[rows_of(lax.rem(b + t, 2) * nl + at)], dst.at[rows_of(t * nl + sender)],
            d_s.at[k, t * nl + dl - 1], d_r.at[k, t * nl + dl - 1], (h, at, b, r),
        )

    def back_start(k, src, dst, t):
        for dl in range(1, nl):
            back(k, src, dst, t, dl, l).start()
        dst[rows_of(t * nl + l), :] = src[rows_of(lax.rem(b + t, 2) * nl + l), :]

    def back_wait(k, src, dst, t):
        for dl in range(1, nl):
            back(k, src, dst, t, dl, lax.rem(l + nl - dl, nl)).wait_recv()

    def info(i):
        return remote((route_t, gates_t)[i], (route_p, gates_p)[i], p_s.at[i], p_r.at[i], y_dev)

    def far_copy(i):
        return remote(far_send.at[i], far_recv.at[i], f_s.at[i], f_r.at[i], y_dev)

    parts = (dw_gate, dw_up, dw_down)
    first_flag, second_flag = flags[l], flags[l + nl]
    final_side = jnp.where(first_flag != second_flag, 1 - h, h)
    keep_mine = jnp.where(final_side == b, 1.0, 0.0).astype(F32)

    def r_grad(w, p, side):
        return remote(
            parts[w].at[shard(side, r_peer(p))], from_r.at[w, p - 1, side],
            g_s.at[w, p - 1, side], g_r.at[w, p - 1, side], (h, l, b, r_peer(p)),
        )

    def y_grad(w, i):
        return remote(
            parts[w].at[shard_piece(1 - b, r, i)], from_y.at[w, piece(i)],
            y_s.at[3 + w, i], y_r.at[3 + w, i], y_dev,
        )

    def y_grad_start(w):
        for i in range(PIECES):
            y_grad(w, i).start()

    def y_grad_sent(w):
        for i in range(PIECES):
            y_grad(w, i).wait_send()

    def z_grad(w, i):
        return remote(
            to_z.at[w, piece(i)], from_z.at[w, piece(i)], z_s.at[3 + w, i], z_r.at[3 + w, i], z_dev
        )

    def grad_r_start(w):
        for side in range(2):
            for p in range(1, nr):
                r_grad(w, p, side).start()

    chunk = min(piece_rows, 64)

    def grad_sum(w):
        for side in range(2):
            for p in range(1, nr):
                r_grad(w, p, side).wait_recv()

        for side in range(2):
            @pl.loop(0, rows // chunk)
            def _(i):
                at = pl.ds(pl.multiple_of((side * nr + r) * rows + i * chunk, chunk), chunk)
                near = tile_at(i, chunk)
                total = parts[w][at, :].astype(F32)
                for p in range(1, nr):
                    total = total + from_r[w, p - 1, side, near, :].astype(F32)
                parts[w][at, :] = total.astype(BF)

    def sides(w, i):
        at = pl.ds(pl.multiple_of((b * nr + r) * rows + i * chunk, chunk), chunk)
        return parts[w][at, :].astype(F32), from_y[w, tile_at(i, chunk), :].astype(F32)

    def grad_z_start(w, which):
        for k in which:
            y_grad(w, k).wait_recv()

            @pl.loop(k * piece_rows // chunk, (k + 1) * piece_rows // chunk)
            def _(i):
                mine, other = sides(w, i)
                to_z[w, tile_at(i, chunk), :] = (mine * (1.0 - keep_mine) + other * keep_mine).astype(BF)
            z_grad(w, k).start()

    def grad_end(w, out):
        for k in range(PIECES):
            z_grad(w, k).wait_recv()

        @pl.loop(0, rows // chunk)
        def _(i):
            mine, other = sides(w, i)
            kept = mine * keep_mine + other * (1.0 - keep_mine)
            out[tile_at(i, chunk), :] = kept + from_z[w, tile_at(i, chunk), :].astype(F32)

    weight_start(0)

    info(0).start()
    info(1).start()
    row_id = lax.broadcasted_iota(jnp.int32, (tok, tok), 0)
    col_id = lax.broadcasted_iota(jnp.int32, (tok, tok), 1)

    def column(line):
        return jnp.sum(jnp.where(row_id == col_id, line, 0.0), axis=1, keepdims=True)

    def slots_of(lines):
        one, two = (column(lines[k : k + 1, :].astype(F32)).astype(jnp.int32) for k in range(2))
        lanes = lax.broadcasted_iota(jnp.int32, (tok, 128), 1)
        match_one, match_two = one == lanes, two == lanes
        named = (jnp.where(match_one, 1.0, 0.0) + jnp.where(match_two, 1.0, 0.0)).astype(BF)
        before = dot(jnp.where(col_id < row_id, 1.0, 0.0).astype(BF), named, 1, 0)
        places = []
        for ids, match in ((one, match_one), (two, match_two)):
            rank = jnp.sum(jnp.where(match, before, 0.0), axis=1, keepdims=True).astype(jnp.int32)
            places.append(ids * cap + rank)
        return places

    for k in range(2):
        gates[:, k : k + 1] = column(gates_t[k : k + 1, :])
    slot_ids = lax.broadcasted_iota(jnp.int32, (tok, slots), 1)
    half = nl * cap
    side_ids = lax.broadcasted_iota(jnp.int32, (tok, half), 1) + b * half
    for k, place in enumerate(slots_of(route_t)):
        pick[k] = jnp.where(place == slot_ids, 1.0, 0.0).astype(BF)
        near[k] = jnp.where(place == side_ids, 1.0, 0.0).astype(BF)
    both = pick[0] + pick[1]

    n_tiles = n_f // TILE
    d_tiles = tokens.shape[1] // TILE
    chosen = both.astype(F32).T.astype(BF)
    read_tokens.wait()

    @pl.loop(0, d_tiles)
    def _(j):
        send_x[:, tile_at(j, TILE)] = dot(chosen, tokens[:, tile_at(j, TILE)], 1, 0).astype(BF)

    exchange_start(0, send_x, recv_x, False)
    exchange_start(0, send_x, recv_x, True)
    weight_start(1)
    weight_start(2)
    read_cot.wait()
    one_t, two_t = pick[0].astype(F32).T.astype(BF), pick[1].astype(F32).T.astype(BF)

    @pl.loop(0, d_tiles)
    def _(j):
        cot = out_grad[:, tile_at(j, TILE)].astype(F32)
        cot_one = (gates[:, 0:1] * cot).astype(BF)
        cot_two = (gates[:, 1:2] * cot).astype(BF)
        send_c[:, tile_at(j, TILE)] = (dot(one_t, cot_one, 1, 0) + dot(two_t, cot_two, 1, 0)).astype(BF)

    exchange_start(1, send_c, recv_c, False)
    weight_z(0, 0)
    weight_z(0, 1)
    exchange_start(1, send_c, recv_c, True)
    weight_y(0)
    weight_r(0)
    exchange_wait(0, send_x, recv_x)

    @pl.loop(0, n_tiles)
    def _(j):
        at = tile_at(j, TILE)
        pre_gate[:, at] = dot(recv_x[...], w_gate[:, at], 1, 0)

    @pl.loop(0, d_tiles)
    def _(j):
        at = tile_at(j, TILE)
        x_t[at, :] = recv_x[:, at].T

    info(0).wait_recv()
    info(1).wait_recv()
    for k in range(2):
        gates_far[:, k : k + 1] = column(gates_p[k : k + 1, :])
    for k, place in enumerate(slots_of(route_p)):
        far[k] = jnp.where(place == side_ids, 1.0, 0.0).astype(BF)

    weight_z(1, 0)
    weight_z(1, 1)
    weight_y(1)
    weight_r(1)

    @pl.loop(0, n_tiles)
    def _(j):
        at = tile_at(j, TILE)
        up = dot(recv_x[...], w_up[:, at], 1, 0)
        gate = pre_gate[:, at]
        pre_up[:, at] = up
        hid = (gate * jax.nn.sigmoid(gate) * up).astype(BF)
        hidden[:, at] = hid
        h_t[at, :] = hid.T

    weight_z(2, 0)
    weight_z(2, 1)
    weight_y(2)
    weight_r(2)

    @pl.loop(0, d_tiles)
    def _(j):
        at = tile_at(j, TILE)
        send_out[:, at] = dot(hidden[...], w_down[:, at], 1, 0).astype(BF)

    back_start(2, send_out, ret_out, 1)
    exchange_wait(1, send_c, recv_c)

    @pl.loop(0, d_tiles)
    def _(j):
        at = tile_at(j, TILE)
        dw_down[:, at] = dot(h_t[...], recv_c[:, at], 1, 0).astype(BF)

    grad_r_start(2)
    grad_sum(2)
    y_grad_start(2)

    @pl.loop(0, n_tiles)
    def _(j):
        at = tile_at(j, TILE)
        grad_h = dot(recv_c[...], w_down[at, :], 1, 1)
        gate, up = pre_gate[:, at], pre_up[:, at]
        sig = jax.nn.sigmoid(gate)
        grad_a[:, at] = (grad_h * up * sig * (1.0 + gate * (1.0 - sig))).astype(BF)
        grad_b[:, at] = (grad_h * gate * sig).astype(BF)


    @pl.loop(0, n_tiles)
    def _(j):
        at = tile_at(j, TILE)
        dw_gate[:, at] = dot(x_t[...], grad_a[:, at], 1, 0).astype(BF)

    grad_r_start(0)
    grad_z_start(2, (0, 1))
    grad_sum(0)
    y_grad_start(0)

    @pl.loop(0, n_tiles)
    def _(j):
        at = tile_at(j, TILE)
        dw_up[:, at] = dot(x_t[...], grad_b[:, at], 1, 0).astype(BF)

    grad_r_start(1)

    @pl.loop(0, d_tiles)
    def _(j):
        at = tile_at(j, TILE)
        send_grad[:, at] = (dot(grad_a[...], w_gate[at, :], 1, 1) + dot(grad_b[...], w_up[at, :], 1, 1)).astype(BF)

    back_start(3, send_grad, ret_grad, 1)
    back_start(2, send_out, ret_out, 0)
    back_start(3, send_grad, ret_grad, 0)
    grad_sum(1)
    y_grad_start(1)
    grad_z_start(0, (0, 1))
    back_wait(2, send_out, ret_out, 1)

    @pl.loop(0, d_tiles)
    def _(j):
        at = tile_at(j, TILE)
        rows_far = ret_out[half:, at]
        far_send[0, :, at] = (
            gates_far[:, 0:1] * dot(far[0], rows_far, 1, 0)
            + gates_far[:, 1:2] * dot(far[1], rows_far, 1, 0)
        ).astype(BF)

    far_copy(0).start()
    grad_z_start(1, (0, 1))
    back_wait(3, send_grad, ret_grad, 1)

    @pl.loop(0, d_tiles)
    def _(j):
        at = tile_at(j, TILE)
        far_send[1, :, at] = dot(far[0] + far[1], ret_grad[half:, at], 1, 0).astype(BF)

    far_copy(1).start()
    back_wait(2, send_out, ret_out, 0)

    @pl.loop(0, d_tiles)
    def _(j):
        at = tile_at(j, TILE)
        rows_near = ret_out[:half, at]
        pre_gate[:tok, at] = (
            gates[:, 0:1] * dot(near[0], rows_near, 1, 0)
            + gates[:, 1:2] * dot(near[1], rows_near, 1, 0)
        )

    back_wait(3, send_grad, ret_grad, 0)

    @pl.loop(0, d_tiles)
    def _(j):
        at = tile_at(j, TILE)
        pre_up[:tok, at] = dot(near[0] + near[1], ret_grad[:half, at], 1, 0)

    grad_end(2, out_down)
    far_copy(0).wait_recv()

    @pl.loop(0, tok // 64)
    def _(i):
        at = tile_at(i, 64)
        layer_out[at, :] = (pre_gate[at, :] + far_recv[0, at, :].astype(F32)).astype(BF)

    grad_end(0, out_gate)
    far_copy(1).wait_recv()

    @pl.loop(0, tok // 64)
    def _(i):
        at = tile_at(i, 64)
        grad_tokens[at, :] = (pre_up[at, :] + far_recv[1, at, :].astype(F32)).astype(BF)

    grad_end(1, out_up)

    for w in range(3):
        y_grad_sent(w)
    for w in range(3):
        for i in range(PIECES):
            z_weight(w, i, relay.at[w, piece(i)]).wait_send()
            y_weight(w, i, ins[w].at[piece(i)], b).wait_send()
            z_grad(w, i).wait_send()
            for p in range(1, nr):
                for group in range(2):
                    r_weight(w, i, group, ins[w].at[piece(i)], b, p, r).wait_send()
        for p in range(1, nr):
            for side in range(2):
                r_grad(w, p, side).wait_send()
    for i in range(2):
        info(i).wait_send()
        far_copy(i).wait_send()
    for k, (src, dst) in enumerate(((send_x, recv_x), (send_c, recv_c))):
        for p in range(1, experts):
            exchange(k, src, dst, p, me).wait_send()
    for k, (src, dst) in ((2, (send_out, ret_out)), (3, (send_grad, ret_grad))):
        for t in range(2):
            for dl in range(1, nl):
                back(k, src, dst, t, dl, l).wait_send()


def store(*refs):
    sources, targets, sems = refs[:5], refs[5:10], refs[10]
    copies = []
    for i in range(5):
        size = sources[i].shape[0] // SPLIT
        for k in range(SPLIT):
            at = pl.ds(k * size, size)
            copies.append(pltpu.make_async_copy(sources[i].at[at], targets[i].at[at], sems.at[i, k]))
    for copy in copies:
        copy.start()
    for copy in copies:
        copy.wait()


def shards(tokens, route_ids, gate_values, w_gate, w_up, w_down, swap_flags, out_grad):
    nl, nr = lax.axis_size("l"), lax.axis_size("r")
    tok, width = tokens.shape
    rows, n_f = w_gate.shape[1:]
    cap = 3 * tok * route_ids.shape[1] // (4 * nl)
    slots = 2 * nl * cap
    wide = 2 * nr * rows
    vmem = pl.BlockSpec(memory_space=pltpu.VMEM)
    hbm = pl.BlockSpec(memory_space=pl.ANY)
    dma = pltpu.SemaphoreType.DMA
    slot_rows = pltpu.VMEM((slots, width), BF)
    slot_f32 = pltpu.VMEM((slots, n_f), F32)
    weight = pltpu.VMEM((wide, n_f), BF)
    step = pl.pallas_call(
        functools.partial(kernel, nl, nr, cap),
        out_shape=(
            pltpu.VMEM((tok, width), BF),
            pltpu.VMEM((tok, width), BF),
            pltpu.VMEM((rows, n_f), F32),
            pltpu.VMEM((rows, n_f), F32),
            pltpu.VMEM((rows, n_f), F32),
        ),
        in_specs=[pl.BlockSpec(memory_space=pltpu.SMEM), hbm, vmem, vmem, hbm, hbm, hbm, hbm],
        out_specs=(vmem,) * 5,
        scratch_shapes=[
            pltpu.VMEM((tok, width), BF), pltpu.VMEM((tok, width), BF),
            dma((2,)),
            pltpu.VMEM((2, tok, slots), BF),
            slot_rows, slot_rows, slot_rows, slot_rows,
            pltpu.VMEM((width, slots), BF), pltpu.VMEM((n_f, slots), BF),
            weight, weight, weight,
            pltpu.VMEM((3, rows, n_f), BF),
            slot_f32, slot_f32,
            slot_rows, slot_rows, slot_rows,
            weight, weight, weight,
            pltpu.VMEM((3, nr - 1, 2, rows, n_f), BF),
            pltpu.VMEM((3, rows, n_f), BF),
            pltpu.VMEM((3, rows, n_f), BF),
            pltpu.VMEM((3, rows, n_f), BF),
            slot_rows, slot_rows, slot_rows, slot_rows,
            pltpu.VMEM((tok, 2), F32), pltpu.VMEM((tok, 2), F32),
            pltpu.VMEM((2, tok, slots // 2), BF), pltpu.VMEM((2, tok, slots // 2), BF),
            pltpu.VMEM((2, tok), jnp.int32), pltpu.VMEM((2, tok), F32),
            pltpu.VMEM((2, tok, width), BF), pltpu.VMEM((2, tok, width), BF),
            dma((6, PIECES)), dma((6, PIECES)), dma((6, PIECES)), dma((6, PIECES)),
            dma((3, PIECES, 2, nr - 1)), dma((3, PIECES, 2, nr - 1)),
            dma((3, nr - 1, 2)), dma((3, nr - 1, 2)),
            dma((4, 2 * nl - 1)), dma((4, 2 * nl - 1)),
            dma((3,)), dma((2,)), dma((2,)), dma((2,)), dma((2,)),
        ],
        compiler_params=pltpu.CompilerParams(
            collective_id=0, has_side_effects=True, vmem_limit_bytes=58 * 2**20
        ),
    )
    outs = step(swap_flags, tokens, route_ids.T, gate_values.T, out_grad, w_gate[0], w_up[0], w_down[0])
    outs = pl.pallas_call(
        store,
        out_shape=tuple(jax.ShapeDtypeStruct(out.shape, out.dtype) for out in outs),
        in_specs=[vmem] * 5,
        out_specs=(hbm,) * 5,
        scratch_shapes=[dma((5, SPLIT))],
        compiler_params=pltpu.CompilerParams(vmem_limit_bytes=2**20),
    )(*(pltpu.with_memory_space_constraint(out, pltpu.VMEM) for out in outs))
    return outs[0], outs[1], outs[2][None], outs[3][None], outs[4][None]


def solution(mesh):
    n_expert, n_dp = mesh.shape["expert"], mesh.shape["dp"]
    split = Mesh(mesh.devices.reshape(2, n_expert // 2, 2, n_dp // 2), ("h", "l", "b", "r"))
    rows = P(("h", "l", "b", "r"), None)
    weight = P(("h", "l"), ("b", "r"), None)
    return jax.shard_map(
        shards,
        mesh=split,
        in_specs=(rows, rows, rows, weight, weight, weight, P(), rows),
        out_specs=(rows, rows, weight, weight, weight),
        check_vma=False,
    )
```
